128 devices in a mesh: section: 4 (over z), scan: 32 (over x, y, core).
Axes of the slice: x: 4, y: 4, z: 4, core: 2. Of those that a mesh axis runs over, the one named last changes fastest.
Arguments:
- frames: bfloat16 [128, 1024, 2048], P('scan', None, 'section'), may hold values from -6 to 6
- increments: int32 [128], P('scan'), may hold values from 1 to 2
- resample: bfloat16 [256, 32, 32], replicated, may hold values from -1 to 2
- wigner_filter: bfloat16 [2, 128, 1024, 2048], P(None, None, ('section', 'scan')), may hold values from -6 to 6
Outputs:
- deconvolved: bfloat16 [2, 128, 1024, 2048], P(None, None, ('section', 'scan'))
The draws below stay inside these ranges and needn't reach their ends.
Inputs may be any that keep to these rules, and one draw needn't show every extreme that they name: `increments`: each scan row advances the descan drift by one or two table entries.
All inputs are finite; a program needn't handle non-finite values.
Results may differ from the reference program's by a relative error of at most 0.0066.
Values may be sent and summed in bfloat16 or wider, within the bound.
A program may use at most 192 MiB of HBM per device.

```python
import math
import jax
import jax.numpy as jnp
from jax import lax

DET_ROWS = 32
DET_COLS = 64
POSITIONS = 1024
PIXELS = 2048
ROWS = 128
SHIFTS = 256


def draw_resample(key, part):
    detector_axis = jnp.arange(DET_ROWS, dtype=jnp.float32)
    offset = 2.0 * (jnp.arange(SHIFTS, dtype=jnp.float32) + 0.5) / SHIFTS - 1.0
    kernel = jnp.sinc(detector_axis[None, :, None] - detector_axis[None, None, :] - offset[:, None, None])
    noise = jnp.clip(jax.random.normal(key, (SHIFTS, DET_ROWS, DET_ROWS), jnp.float32), -4.0, 4.0)
    return (kernel + noise * (0.5 / math.sqrt(DET_ROWS))).astype(jnp.bfloat16)


def place_ends(result, stream_key, least, top_value):
    longest = result.shape.index(max(result.shape))
    spots = []
    for shift in (0, 1):
        where = [jax.random.randint(jax.random.fold_in(stream_key, axis), (), 0, length) for axis, length in enumerate(result.shape)]
        where[longest] = (where[longest] + shift) % result.shape[longest]
        spots.append(tuple(where))
    return result.at[spots[0]].set(least).at[spots[1]].set(top_value)


def levels(own_key, extent, shards, smallest, high):
    def one(axis_at, shards_of):
        steps = jax.random.uniform(jax.random.fold_in(jax.random.fold_in(own_key, 6), axis_at), (shards_of,), jnp.float32, smallest / len(shards), high / len(shards))
        return jnp.repeat(jnp.exp(steps), extent[axis_at] // shards_of).reshape((-1,) + (1,) * (len(extent) - axis_at - 1))

    factor_of = one(*shards[0])
    for cut in shards[1:]:
        factor_of = factor_of * one(*cut)
    return factor_of


def centred(key, extent, width, most, pieces=(), kind=jnp.bfloat16):
    gain = levels(key, extent, pieces, -0.22, 0.18) if pieces else 1.0
    values = jax.random.normal(key, extent, jnp.float32) * width * gain
    return jnp.minimum(jnp.maximum(values, -most), most).astype(kind)


def setup_inputs(seed: int = 0) -> dict:
    key_of = jax.random.split(jax.random.key(seed), 5)
    frames = centred(key_of[0], (ROWS, POSITIONS, PIXELS), 1.0, 6.0, ((0, 32), (2, 4)))
    increments = place_ends(jax.random.randint(key_of[1], (ROWS,), 1, 3), jax.random.fold_in(key_of[1], 1), 1, 2).astype(jnp.int32)
    resample = draw_resample(jax.random.fold_in(key_of[4], 71), 0)
    wigner_filter = centred(key_of[3], (2, ROWS, POSITIONS, PIXELS), 1.0, 6.0, ((2, 128),))
    return {"frames": frames, "increments": increments, "resample": resample, "wigner_filter": wigner_filter}


def fast_matrix(length):
    steps_p = jnp.arange(length, dtype=jnp.int32)
    phase = steps_p[:, None] * steps_p[None, :] % length
    angle = phase.astype(jnp.float32) * (2.0 * math.pi / length)
    return jnp.concatenate([jnp.cos(angle), -jnp.sin(angle)], axis=0).astype(jnp.bfloat16)

def slow_matrix(row_order, length):
    frequency = jnp.arange(length, dtype=jnp.int32)
    phase = frequency[:, None] * row_order[None, :] % length
    angle = phase.astype(jnp.float32) * (2.0 * math.pi / length)
    cosine = jnp.cos(angle)
    sine = jnp.sin(angle)
    upper = jnp.stack([cosine, sine], axis=1)
    lower = jnp.stack([-sine, cosine], axis=1)
    return jnp.stack([upper, lower], axis=0).astype(jnp.bfloat16)

def reference(frames, increments, resample, wigner_filter):
    shift_index = (jnp.cumsum(increments).astype(jnp.int32) - 1).astype(jnp.int32)
    matrices = resample[shift_index]
    fast_table = fast_matrix(POSITIONS)

    def row_spectrum(operands):
        frame_row, matrix = operands
        raw = jnp.dot(fast_table, frame_row, preferred_element_type=jnp.float32)
        raw = (raw * (1.0 / math.sqrt(POSITIONS))).astype(jnp.bfloat16)
        blocked = raw.astype(jnp.float32).reshape(2, POSITIONS, DET_ROWS, DET_COLS)
        shifted = jnp.einsum('ab,cpbx->cpax', matrix.astype(jnp.float32), blocked)
        return shifted.reshape(2, POSITIONS, PIXELS).astype(jnp.bfloat16)
    spectrum = lax.map(row_spectrum, (frames, matrices))
    slow_table = slow_matrix(jnp.arange(ROWS, dtype=jnp.int32), ROWS).reshape(2 * ROWS, 2 * ROWS)
    block_width = math.gcd(PIXELS, 256)
    block_count = PIXELS // block_width
    blocks = spectrum.reshape(ROWS, 2, POSITIONS, block_count, block_width).transpose(3, 1, 0, 2, 4)
    filter_blocks = wigner_filter.reshape(2, ROWS, POSITIONS, block_count, block_width).transpose(3, 0, 1, 2, 4)

    def transform(operands):
        piece_in, filter_piece = operands
        flat = piece_in.reshape(2 * ROWS, POSITIONS * block_width)
        slow_grid = jnp.dot(slow_table, flat, preferred_element_type=jnp.float32) * (1.0 / math.sqrt(ROWS))
        slow_grid = slow_grid.reshape(2, ROWS, POSITIONS, block_width)
        filter_real = filter_piece[0].astype(jnp.float32)
        filter_imag = filter_piece[1].astype(jnp.float32)
        real_part = slow_grid[0] * filter_real - slow_grid[1] * filter_imag
        imag_part = slow_grid[0] * filter_imag + slow_grid[1] * filter_real
        return jnp.stack([real_part, imag_part]).astype(jnp.bfloat16)
    results = lax.map(transform, (blocks, filter_blocks))
    return results.transpose(1, 2, 3, 0, 4).reshape(2, ROWS, POSITIONS, PIXELS)
```

```python
import math

import jax
import jax.numpy as jnp
from jax import lax
from jax.sharding import PartitionSpec as P


def fast_matrix(length):
    steps_p = jnp.arange(length, dtype=jnp.int32)
    phase = steps_p[:, None] * steps_p[None, :] % length
    angle = phase.astype(jnp.float32) * (2.0 * math.pi / length)
    return jnp.stack([jnp.cos(angle), -jnp.sin(angle)], axis=0).astype(jnp.bfloat16)


def slow_matrix(row_order, length):
    frequency = jnp.arange(length, dtype=jnp.int32)
    phase = frequency[:, None] * row_order[None, :] % length
    angle = phase.astype(jnp.float32) * (2.0 * math.pi / length)
    cosine = jnp.cos(angle)
    sine = jnp.sin(angle)
    upper = jnp.stack([cosine, sine], axis=1)
    lower = jnp.stack([-sine, cosine], axis=1)
    return jnp.stack([upper, lower], axis=0).astype(jnp.bfloat16)


def shards(frames, increments, resample, wigner_filter):
    section_count = lax.axis_size("section")
    scan_count = lax.axis_size("scan")
    devices = section_count * scan_count
    rows_loc, positions, pixels_loc = frames.shape
    total_rows = rows_loc * scan_count
    detector_rows = resample.shape[1]
    rows_sec = detector_rows // section_count
    detector_cols = pixels_loc // rows_sec
    q_loc = positions // devices

    fast_table = fast_matrix(positions).reshape(2, devices, q_loc, positions)
    raw = jnp.einsum("cdqp,rpk->dcqrk", fast_table, frames, preferred_element_type=jnp.float32)
    raw = (raw * (1.0 / math.sqrt(positions))).astype(jnp.bfloat16)
    got = lax.all_to_all(raw, ("section", "scan"), 0, 0, tiled=True)
    got = got.reshape(section_count, scan_count, 2, q_loc, rows_loc, rows_sec, detector_cols)

    every_increment = lax.all_gather(increments, "scan", tiled=True)
    shift_index = jnp.cumsum(every_increment) - 1
    matrices = resample[shift_index].reshape(scan_count, rows_loc, detector_rows, section_count, rows_sec)
    spectrum = jnp.einsum("jiasb,sjcqibx->cqjiax", matrices, got, preferred_element_type=jnp.float32)
    spectrum = spectrum.astype(jnp.bfloat16).reshape(2, q_loc, total_rows, detector_rows * detector_cols)

    slow_table = slow_matrix(jnp.arange(total_rows, dtype=jnp.int32), total_rows)
    slow_grid = jnp.einsum("aybr,bqrk->ayqk", slow_table, spectrum, preferred_element_type=jnp.float32)
    slow_grid = slow_grid * (1.0 / math.sqrt(total_rows))
    filter_real = wigner_filter[0].astype(jnp.float32)
    filter_imag = wigner_filter[1].astype(jnp.float32)
    real_part = slow_grid[0] * filter_real - slow_grid[1] * filter_imag
    imag_part = slow_grid[0] * filter_imag + slow_grid[1] * filter_real
    return jnp.stack([real_part, imag_part]).astype(jnp.bfloat16)


def solution(mesh):
    in_specs = (
        P("scan", None, "section"),
        P("scan"),
        P(),
        P(None, None, ("section", "scan"), None),
    )
    out_specs = P(None, None, ("section", "scan"), None)
    return jax.shard_map(shards, mesh=mesh, in_specs=in_specs, out_specs=out_specs, check_vma=False)
```

```python
import math

import jax
import jax.numpy as jnp
from jax import lax
from jax.sharding import PartitionSpec as P

CHUNKS = 2


def fast_matrix(length):
    steps_p = jnp.arange(length, dtype=jnp.int32)
    phase = steps_p[:, None] * steps_p[None, :] % length
    angle = phase.astype(jnp.float32) * (2.0 * math.pi / length)
    return jnp.stack([jnp.cos(angle), -jnp.sin(angle)], axis=0).astype(jnp.bfloat16)


def slow_matrix(row_order, length):
    frequency = jnp.arange(length, dtype=jnp.int32)
    phase = frequency[:, None] * row_order[None, :] % length
    angle = phase.astype(jnp.float32) * (2.0 * math.pi / length)
    cosine = jnp.cos(angle)
    sine = jnp.sin(angle)
    upper = jnp.stack([cosine, sine], axis=1)
    lower = jnp.stack([-sine, cosine], axis=1)
    return jnp.stack([upper, lower], axis=0).astype(jnp.bfloat16)


def shards(frames, increments, resample, wigner_filter):
    section_count = lax.axis_size("section")
    scan_count = lax.axis_size("scan")
    devices = section_count * scan_count
    rows_loc, positions, pixels_loc = frames.shape
    total_rows = rows_loc * scan_count
    detector_rows = resample.shape[1]
    rows_sec = detector_rows // section_count
    detector_cols = pixels_loc // rows_sec
    q_loc = positions // devices
    chunk_q = q_loc // CHUNKS

    spread = jnp.broadcast_to(increments[None, :], (scan_count, rows_loc))
    every_increment = lax.all_to_all(spread, "scan", 0, 0, tiled=True).reshape(-1)
    shift_index = jnp.cumsum(every_increment) - 1
    matrices = resample[shift_index].reshape(scan_count, rows_loc, detector_rows, section_count, rows_sec)

    fast_table = fast_matrix(positions).reshape(2, devices, CHUNKS, chunk_q, positions)
    slow_table = slow_matrix(jnp.arange(total_rows, dtype=jnp.int32), total_rows)
    sign = jnp.array([-1.0, 1.0], jnp.float32).reshape(2, 1, 1, 1)
    pieces = []
    for h in range(CHUNKS):
        raw = jnp.einsum("cdqp,rpk->dcqrk", fast_table[:, :, h], frames, preferred_element_type=jnp.float32)
        raw = (raw * (1.0 / math.sqrt(positions))).astype(jnp.bfloat16)
        got = lax.all_to_all(raw, ("section", "scan"), 0, 0, tiled=True)
        got = got.reshape(section_count, scan_count, 2, chunk_q, rows_loc, rows_sec, detector_cols)
        spectrum = jnp.einsum("jiasb,sjcqibx->cqjiax", matrices, got, preferred_element_type=jnp.float32)
        spectrum = spectrum.astype(jnp.bfloat16).reshape(2, chunk_q, total_rows, detector_rows * detector_cols)
        slow_grid = jnp.einsum("aybr,bqrk->ayqk", slow_table, spectrum, preferred_element_type=jnp.float32)
        slow_grid = slow_grid * (1.0 / math.sqrt(total_rows))
        gains = wigner_filter[:, :, h * chunk_q:(h + 1) * chunk_q].astype(jnp.float32)
        pieces.append((slow_grid[0:1] * gains + sign * (slow_grid[1:2] * gains[::-1])).astype(jnp.bfloat16))
    return jnp.concatenate(pieces, axis=2)


def solution(mesh):
    in_specs = (
        P("scan", None, "section"),
        P("scan"),
        P(),
        P(None, None, ("section", "scan"), None),
    )
    out_specs = P(None, None, ("section", "scan"), None)
    return jax.shard_map(shards, mesh=mesh, in_specs=in_specs, out_specs=out_specs, check_vma=False)
```

```python
import math

import jax
import jax.numpy as jnp
from jax.experimental import pallas as pl
from jax.experimental.pallas import tpu as pltpu
from jax import lax
from jax.sharding import PartitionSpec as P

CHUNKS = 2


def fast_matrix(length):
    steps_p = jnp.arange(length, dtype=jnp.int32)
    phase = steps_p[:, None] * steps_p[None, :] % length
    angle = phase.astype(jnp.float32) * (2.0 * math.pi / length)
    return jnp.stack([jnp.cos(angle), -jnp.sin(angle)], axis=0).astype(jnp.bfloat16)


def slow_matrix(row_order, length):
    frequency = jnp.arange(length, dtype=jnp.int32)
    phase = frequency[:, None] * row_order[None, :] % length
    angle = phase.astype(jnp.float32) * (2.0 * math.pi / length)
    cosine = jnp.cos(angle)
    sine = jnp.sin(angle)
    upper = jnp.stack([cosine, sine], axis=1)
    lower = jnp.stack([-sine, cosine], axis=1)
    return jnp.stack([upper, lower], axis=0).astype(jnp.bfloat16)


def slow_kernel(table_ref, spectrum_ref, gains_ref, out_ref, gains_wide, out_wide, *, scale):
    q_loc = spectrum_ref.shape[0]
    half = gains_ref.shape[1] // q_loc
    table = table_ref[...]
    gains_wide[...] = gains_ref[...].astype(jnp.float32)
    for q in range(q_loc):
        rows = pl.ds(q, half, stride=q_loc)
        grid = jnp.dot(table, spectrum_ref[q], preferred_element_type=jnp.float32) * scale
        grid_real = grid[:half]
        grid_imag = grid[half:]
        gain_real = gains_wide[0, rows, :]
        gain_imag = gains_wide[1, rows, :]
        out_wide[0, rows, :] = grid_real * gain_real - grid_imag * gain_imag
        out_wide[1, rows, :] = grid_real * gain_imag + grid_imag * gain_real
    out_ref[...] = out_wide[...].astype(out_ref.dtype)


def slow_and_filter(table, spectrum, wigner_filter, scale):
    q_loc, depth, pixels = spectrum.shape
    shape = wigner_filter.shape
    flat = wigner_filter.reshape(shape[0], shape[1] * shape[2], shape[3])
    block = 128
    out = pl.pallas_call(
        lambda *refs: slow_kernel(*refs, scale=scale),
        grid=(pixels // block,),
        in_specs=[
            pl.BlockSpec((depth, depth), lambda j: (0, 0)),
            pl.BlockSpec((q_loc, depth, block), lambda j: (0, 0, j)),
            pl.BlockSpec((2, flat.shape[1], block), lambda j: (0, 0, j)),
        ],
        out_specs=pl.BlockSpec((2, flat.shape[1], block), lambda j: (0, 0, j)),
        out_shape=jax.ShapeDtypeStruct(flat.shape, jnp.bfloat16),
        scratch_shapes=[pltpu.VMEM((2, flat.shape[1], block), jnp.float32)] * 2,
    )(table, spectrum, flat)
    return out.reshape(shape)


def shards(frames, increments, resample, wigner_filter):
    section_count = lax.axis_size("section")
    scan_count = lax.axis_size("scan")
    devices = section_count * scan_count
    rows_loc, positions, pixels_loc = frames.shape
    total_rows = rows_loc * scan_count
    detector_rows = resample.shape[1]
    rows_sec = detector_rows // section_count
    detector_cols = pixels_loc // rows_sec
    q_loc = positions // devices
    chunk_q = q_loc // CHUNKS

    spread = jnp.broadcast_to(increments[None, :], (scan_count, rows_loc))
    every_increment = lax.all_to_all(spread, "scan", 0, 0, tiled=True).reshape(-1)
    shift_index = jnp.cumsum(every_increment) - 1
    matrices = resample[shift_index].reshape(scan_count, rows_loc, detector_rows, section_count, rows_sec)

    fast_table = fast_matrix(positions).reshape(2, devices, CHUNKS, chunk_q, positions)
    pieces = []
    for h in range(CHUNKS):
        raw = jnp.einsum("cdqp,rpk->dcqrk", fast_table[:, :, h], frames, preferred_element_type=jnp.float32)
        raw = (raw * (1.0 / math.sqrt(positions))).astype(jnp.bfloat16)
        got = lax.all_to_all(raw, ("section", "scan"), 0, 0, tiled=True)
        got = got.reshape(section_count, scan_count, 2, chunk_q, rows_loc, rows_sec, detector_cols)
        spectrum = jnp.einsum("jiasb,sjcqibx->qcjiax", matrices, got, preferred_element_type=jnp.float32)
        pieces.append(spectrum.astype(jnp.bfloat16).reshape(chunk_q, 2 * total_rows, detector_rows * detector_cols))
    spectrum = jnp.concatenate(pieces, axis=0)
    slow_table = slow_matrix(jnp.arange(total_rows, dtype=jnp.int32), total_rows).reshape(2 * total_rows, 2 * total_rows)
    return slow_and_filter(slow_table, spectrum, wigner_filter, 1.0 / math.sqrt(total_rows))


def solution(mesh):
    in_specs = (
        P("scan", None, "section"),
        P("scan"),
        P(),
        P(None, None, ("section", "scan"), None),
    )
    out_specs = P(None, None, ("section", "scan"), None)
    return jax.shard_map(shards, mesh=mesh, in_specs=in_specs, out_specs=out_specs, check_vma=False)
```

```python
import math

import jax
import jax.numpy as jnp
from jax.experimental import pallas as pl
from jax.experimental.pallas import tpu as pltpu
from jax import lax
from jax.sharding import PartitionSpec as P

CHUNKS = 2


def fast_matrix(length):
    steps_p = jnp.arange(length, dtype=jnp.int32)
    phase = steps_p[:, None] * steps_p[None, :] % length
    angle = phase.astype(jnp.float32) * (2.0 * math.pi / length)
    return jnp.stack([jnp.cos(angle), -jnp.sin(angle)], axis=0).astype(jnp.bfloat16)


def slow_matrix(row_order, length):
    frequency = jnp.arange(length, dtype=jnp.int32)
    phase = frequency[:, None] * row_order[None, :] % length
    angle = phase.astype(jnp.float32) * (2.0 * math.pi / length)
    cosine = jnp.cos(angle)
    sine = jnp.sin(angle)
    upper = jnp.stack([cosine, sine], axis=1)
    lower = jnp.stack([-sine, cosine], axis=1)
    return jnp.stack([upper, lower], axis=0).astype(jnp.bfloat16)


def slow_kernel(table_ref, *refs, scale, chunks):
    spectrum_refs = refs[:chunks]
    gains_ref, out_ref, gains_wide, out_wide, spectrum_wide = refs[chunks:]
    chunk_q = spectrum_refs[0].shape[0] // table_ref.shape[1]
    q_loc = chunk_q * chunks
    half = gains_ref.shape[1] // q_loc
    depth = table_ref.shape[1]
    table = table_ref[...]
    gains_wide[...] = gains_ref[...].astype(jnp.float32)
    for h in range(chunks):
        spectrum_wide[...] = spectrum_refs[h][...].astype(jnp.float32)
        for k in range(chunk_q):
            q = h * chunk_q + k
            rows = pl.ds(q, half, stride=q_loc)
            columns = spectrum_wide[pl.ds(k, depth, stride=chunk_q), :].astype(jnp.bfloat16)
            grid = jnp.dot(table, columns, preferred_element_type=jnp.float32) * scale
            grid_real = grid[:half]
            grid_imag = grid[half:]
            gain_real = gains_wide[0, rows, :]
            gain_imag = gains_wide[1, rows, :]
            out_wide[0, rows, :] = grid_real * gain_real - grid_imag * gain_imag
            out_wide[1, rows, :] = grid_real * gain_imag + grid_imag * gain_real
    out_ref[...] = out_wide[...].astype(out_ref.dtype)


def slow_and_filter(table, pieces, wigner_filter, scale):
    rows, pixels = pieces[0].shape
    shape = wigner_filter.shape
    flat = wigner_filter.reshape(shape[0], shape[1] * shape[2], shape[3])
    block = 128
    depth = table.shape[1]
    chunks = len(pieces)
    out = pl.pallas_call(
        lambda *refs: slow_kernel(*refs, scale=scale, chunks=chunks),
        grid=(pixels // block,),
        in_specs=[pl.BlockSpec((depth, depth), lambda j: (0, 0))]
        + [pl.BlockSpec((rows, block), lambda j: (0, j))] * chunks
        + [pl.BlockSpec((2, flat.shape[1], block), lambda j: (0, 0, j))],
        out_specs=pl.BlockSpec((2, flat.shape[1], block), lambda j: (0, 0, j)),
        out_shape=jax.ShapeDtypeStruct(flat.shape, jnp.bfloat16),
        scratch_shapes=[pltpu.VMEM((2, flat.shape[1], block), jnp.float32)] * 2
        + [pltpu.VMEM((rows, block), jnp.float32)],
    )(table, *pieces, flat)
    return out.reshape(shape)


def shards(frames, increments, resample, wigner_filter):
    section_count = lax.axis_size("section")
    scan_count = lax.axis_size("scan")
    devices = section_count * scan_count
    rows_loc, positions, pixels_loc = frames.shape
    total_rows = rows_loc * scan_count
    detector_rows = resample.shape[1]
    rows_sec = detector_rows // section_count
    detector_cols = pixels_loc // rows_sec
    q_loc = positions // devices
    chunk_q = q_loc // CHUNKS

    spread = jnp.broadcast_to(increments[None, :], (scan_count, rows_loc))
    every_increment = lax.all_to_all(spread, "scan", 0, 0, tiled=True).reshape(-1)
    shift_index = jnp.cumsum(every_increment) - 1
    matrices = resample[shift_index].reshape(scan_count, rows_loc, detector_rows, section_count, rows_sec)

    steps_p = jnp.arange(positions, dtype=jnp.int32)
    pieces = []
    for h in range(CHUNKS):
        steps_q = (jnp.arange(devices, dtype=jnp.int32)[:, None] * q_loc + h * chunk_q
                   + jnp.arange(chunk_q, dtype=jnp.int32)[None, :])
        phase = steps_q[:, :, None] * steps_p[None, None, :] % positions
        angle = phase.astype(jnp.float32) * (2.0 * math.pi / positions)
        fast_table = jnp.stack([jnp.cos(angle), -jnp.sin(angle)], axis=0).astype(jnp.bfloat16)
        raw = jnp.einsum("cdqp,rpk->dcqrk", fast_table, frames, preferred_element_type=jnp.float32)
        raw = (raw * (1.0 / math.sqrt(positions))).astype(jnp.bfloat16)
        got = lax.all_to_all(raw, ("section", "scan"), 0, 0, tiled=True)
        got = got.reshape(section_count, scan_count, 2, chunk_q, rows_loc, rows_sec, detector_cols)
        spectrum = jnp.einsum("jiasb,sjcqibx->jicqax", matrices, got, preferred_element_type=jnp.float32)
        pieces.append(spectrum.astype(jnp.bfloat16).reshape(total_rows * 2 * chunk_q, detector_rows * detector_cols))
    slow_table = slow_matrix(jnp.arange(total_rows, dtype=jnp.int32), total_rows)
    slow_table = slow_table.transpose(0, 1, 3, 2).reshape(2 * total_rows, 2 * total_rows)
    return slow_and_filter(slow_table, pieces, wigner_filter, 1.0 / math.sqrt(total_rows))


def solution(mesh):
    in_specs = (
        P("scan", None, "section"),
        P("scan"),
        P(),
        P(None, None, ("section", "scan"), None),
    )
    out_specs = P(None, None, ("section", "scan"), None)
    return jax.shard_map(shards, mesh=mesh, in_specs=in_specs, out_specs=out_specs, check_vma=False)
```

```python
import math

import jax
import jax.numpy as jnp
from jax.experimental import pallas as pl
from jax.experimental.pallas import tpu as pltpu
from jax import lax
from jax.sharding import PartitionSpec as P

CHUNKS = 2


def fast_matrix(length):
    steps_p = jnp.arange(length, dtype=jnp.int32)
    phase = steps_p[:, None] * steps_p[None, :] % length
    angle = phase.astype(jnp.float32) * (2.0 * math.pi / length)
    return jnp.stack([jnp.cos(angle), -jnp.sin(angle)], axis=0).astype(jnp.bfloat16)


def slow_matrix(row_order, length):
    frequency = jnp.arange(length, dtype=jnp.int32)
    phase = frequency[:, None] * row_order[None, :] % length
    angle = phase.astype(jnp.float32) * (2.0 * math.pi / length)
    cosine = jnp.cos(angle)
    sine = jnp.sin(angle)
    upper = jnp.stack([cosine, sine], axis=1)
    lower = jnp.stack([-sine, cosine], axis=1)
    return jnp.stack([upper, lower], axis=0).astype(jnp.bfloat16)


def slow_kernel(table_ref, spectrum_ref, gains_ref, *refs, scale, first, q_loc, initial):
    if initial:
        out_ref, gains_wide, out_wide, spectrum_wide = refs
        out_wide[...] = jnp.zeros(out_wide.shape, jnp.float32)
    else:
        earlier_ref, out_ref, gains_wide, out_wide, spectrum_wide = refs
        out_wide[...] = earlier_ref[...].astype(jnp.float32)
    depth = table_ref.shape[1]
    chunk_q = spectrum_ref.shape[0] // depth
    half = gains_ref.shape[1] // q_loc
    table = table_ref[...]
    gains_wide[...] = gains_ref[...].astype(jnp.float32)
    spectrum_wide[...] = spectrum_ref[...].astype(jnp.float32)
    for k in range(chunk_q):
        q = first + k
        rows = pl.ds(q, half, stride=q_loc)
        columns = spectrum_wide[pl.ds(k, depth, stride=chunk_q), :].astype(jnp.bfloat16)
        grid = jnp.dot(table, columns, preferred_element_type=jnp.float32) * scale
        grid_real = grid[:half]
        grid_imag = grid[half:]
        gain_real = gains_wide[0, rows, :]
        gain_imag = gains_wide[1, rows, :]
        out_wide[0, rows, :] = grid_real * gain_real - grid_imag * gain_imag
        out_wide[1, rows, :] = grid_real * gain_imag + grid_imag * gain_real
    out_ref[...] = out_wide[...].astype(out_ref.dtype)


def slow_and_filter(table, spectrum, flat, earlier, first, q_loc, scale):
    rows, pixels = spectrum.shape
    block = 128
    depth = table.shape[1]
    wide = pl.BlockSpec((2, flat.shape[1], block), lambda j: (0, 0, j))
    in_specs = [pl.BlockSpec((depth, depth), lambda j: (0, 0)), pl.BlockSpec((rows, block), lambda j: (0, j)), wide]
    operands = [table, spectrum, flat]
    aliases = {}
    if earlier is not None:
        in_specs.append(wide)
        operands.append(earlier)
        aliases = {3: 0}
    return pl.pallas_call(
        lambda *refs: slow_kernel(*refs, scale=scale, first=first, q_loc=q_loc, initial=earlier is None),
        grid=(pixels // block,),
        in_specs=in_specs,
        out_specs=wide,
        out_shape=jax.ShapeDtypeStruct(flat.shape, jnp.bfloat16),
        scratch_shapes=[pltpu.VMEM((2, flat.shape[1], block), jnp.float32)] * 2
        + [pltpu.VMEM((rows, block), jnp.float32)],
        input_output_aliases=aliases,
        cost_estimate=pl.CostEstimate(flops=2 * depth * depth * rows // depth * pixels, transcendentals=0, bytes_accessed=3 * flat.size * 2),
    )(*operands)


def shards(frames, increments, resample, wigner_filter):
    section_count = lax.axis_size("section")
    scan_count = lax.axis_size("scan")
    devices = section_count * scan_count
    rows_loc, positions, pixels_loc = frames.shape
    total_rows = rows_loc * scan_count
    detector_rows = resample.shape[1]
    rows_sec = detector_rows // section_count
    detector_cols = pixels_loc // rows_sec
    q_loc = positions // devices
    chunk_q = q_loc // CHUNKS

    spread = jnp.broadcast_to(increments[None, :], (scan_count, rows_loc))
    every_increment = lax.all_to_all(spread, "scan", 0, 0, tiled=True).reshape(-1)
    shift_index = jnp.cumsum(every_increment) - 1
    matrices = resample[shift_index].reshape(scan_count, rows_loc, detector_rows, section_count, rows_sec)

    steps_p = jnp.arange(positions, dtype=jnp.int32)
    slow_table = slow_matrix(jnp.arange(total_rows, dtype=jnp.int32), total_rows)
    slow_table = slow_table.transpose(0, 1, 3, 2).reshape(2 * total_rows, 2 * total_rows)
    shape = wigner_filter.shape
    flat = wigner_filter.reshape(shape[0], shape[1] * shape[2], shape[3])
    out = None
    for h in range(CHUNKS):
        steps_q = (jnp.arange(devices, dtype=jnp.int32)[:, None] * q_loc + h * chunk_q
                   + jnp.arange(chunk_q, dtype=jnp.int32)[None, :])
        phase = steps_q[:, :, None] * steps_p[None, None, :] % positions
        angle = phase.astype(jnp.float32) * (2.0 * math.pi / positions)
        fast_table = jnp.stack([jnp.cos(angle), -jnp.sin(angle)], axis=0).astype(jnp.bfloat16)
        raw = jnp.einsum("cdqp,rpk->dcqrk", fast_table, frames, preferred_element_type=jnp.float32)
        raw = (raw * (1.0 / math.sqrt(positions))).astype(jnp.bfloat16)
        got = lax.all_to_all(raw, ("section", "scan"), 0, 0, tiled=True)
        mixing = matrices
        if out is not None:
            mixing, out = lax.optimization_barrier((matrices, out))
        got = got.reshape(section_count, scan_count, 2, chunk_q, rows_loc, rows_sec, detector_cols)
        spectrum = jnp.einsum("jiasb,sjcqibx->jicqax", mixing, got, preferred_element_type=jnp.float32)
        spectrum = spectrum.astype(jnp.bfloat16).reshape(total_rows * 2 * chunk_q, detector_rows * detector_cols)
        out = slow_and_filter(slow_table, spectrum, flat, out, h * chunk_q, q_loc, 1.0 / math.sqrt(total_rows))
    return out.reshape(shape)


def solution(mesh):
    in_specs = (
        P("scan", None, "section"),
        P("scan"),
        P(),
        P(None, None, ("section", "scan"), None),
    )
    out_specs = P(None, None, ("section", "scan"), None)
    return jax.shard_map(shards, mesh=mesh, in_specs=in_specs, out_specs=out_specs, check_vma=False)
```

```python
import math

import jax
import jax.numpy as jnp
from jax.experimental import pallas as pl
from jax.experimental.pallas import tpu as pltpu
from jax import lax
from jax.sharding import PartitionSpec as P

CHUNKS = 2


def fast_matrix(length):
    steps_p = jnp.arange(length, dtype=jnp.int32)
    phase = steps_p[:, None] * steps_p[None, :] % length
    angle = phase.astype(jnp.float32) * (2.0 * math.pi / length)
    return jnp.stack([jnp.cos(angle), -jnp.sin(angle)], axis=0).astype(jnp.bfloat16)


def fast_rows(steps_q, length):
    low = 32
    steps_low = jnp.arange(low, dtype=jnp.int32)
    steps_high = jnp.arange(length // low, dtype=jnp.int32) * low
    scale = 2.0 * math.pi / length
    angle_high = (steps_q[..., None] * steps_high % length).astype(jnp.float32) * scale
    angle_low = (steps_q[..., None] * steps_low % length).astype(jnp.float32) * scale
    cos_high, sin_high = jnp.cos(angle_high)[..., :, None], jnp.sin(angle_high)[..., :, None]
    cos_low, sin_low = jnp.cos(angle_low)[..., None, :], jnp.sin(angle_low)[..., None, :]
    cosine = cos_high * cos_low - sin_high * sin_low
    sine = sin_high * cos_low + cos_high * sin_low
    table = jnp.stack([cosine, -sine], axis=0)
    return table.reshape(table.shape[:-2] + (length,)).astype(jnp.bfloat16)


def slow_matrix(row_order, length):
    frequency = jnp.arange(length, dtype=jnp.int32)
    phase = frequency[:, None] * row_order[None, :] % length
    angle = phase.astype(jnp.float32) * (2.0 * math.pi / length)
    cosine = jnp.cos(angle)
    sine = jnp.sin(angle)
    upper = jnp.stack([cosine, sine], axis=1)
    lower = jnp.stack([-sine, cosine], axis=1)
    return jnp.stack([upper, lower], axis=0).astype(jnp.bfloat16)


def slow_kernel(table_ref, *refs, scale, chunks):
    spectrum_refs = refs[:chunks]
    gains_ref, out_ref, out_wide = refs[chunks:]
    chunk_q = spectrum_refs[0].shape[0] // table_ref.shape[1]
    q_loc = chunk_q * chunks
    half = gains_ref.shape[1] // q_loc
    depth = table_ref.shape[1]
    table = table_ref[...]
    for h in range(chunks):
        for k in range(chunk_q):
            q = h * chunk_q + k
            rows = pl.ds(q, half, stride=q_loc)
            columns = spectrum_refs[h][pl.ds(k, depth, stride=chunk_q), :]
            grid = jnp.dot(table, columns, preferred_element_type=jnp.float32) * scale
            grid_real = grid[:half]
            grid_imag = grid[half:]
            gain_real = gains_ref[0, rows, :].astype(jnp.float32)
            gain_imag = gains_ref[1, rows, :].astype(jnp.float32)
            out_wide[0, rows, :] = grid_real * gain_real - grid_imag * gain_imag
            out_wide[1, rows, :] = grid_real * gain_imag + grid_imag * gain_real
    out_ref[...] = out_wide[...].astype(out_ref.dtype)


def slow_and_filter(table, pieces, wigner_filter, scale):
    rows, pixels = pieces[0].shape
    shape = wigner_filter.shape
    flat = wigner_filter.reshape(shape[0], shape[1] * shape[2], shape[3])
    block = 128
    depth = table.shape[1]
    chunks = len(pieces)
    out = pl.pallas_call(
        lambda *refs: slow_kernel(*refs, scale=scale, chunks=chunks),
        grid=(pixels // block,),
        in_specs=[pl.BlockSpec((depth, depth), lambda j: (0, 0))]
        + [pl.BlockSpec((rows, block), lambda j: (0, j))] * chunks
        + [pl.BlockSpec((2, flat.shape[1], block), lambda j: (0, 0, j))],
        out_specs=pl.BlockSpec((2, flat.shape[1], block), lambda j: (0, 0, j)),
        out_shape=jax.ShapeDtypeStruct(flat.shape, jnp.bfloat16),
        scratch_shapes=[pltpu.VMEM((2, flat.shape[1], block), jnp.float32)],
    )(table, *pieces, flat)
    return out.reshape(shape)


def shards(frames, increments, resample, wigner_filter):
    section_count = lax.axis_size("section")
    scan_count = lax.axis_size("scan")
    devices = section_count * scan_count
    rows_loc, positions, pixels_loc = frames.shape
    total_rows = rows_loc * scan_count
    detector_rows = resample.shape[1]
    rows_sec = detector_rows // section_count
    detector_cols = pixels_loc // rows_sec
    q_loc = positions // devices
    chunk_q = q_loc // CHUNKS

    spread = jnp.broadcast_to(increments[None, :], (scan_count, rows_loc))
    every_increment = lax.all_to_all(spread, "scan", 0, 0, tiled=True).reshape(-1)
    shift_index = jnp.cumsum(every_increment) - 1
    matrices = resample[shift_index].reshape(scan_count, rows_loc, detector_rows, section_count, rows_sec)

    pieces = []
    for h in range(CHUNKS):
        steps_q = (jnp.arange(devices, dtype=jnp.int32)[:, None] * q_loc + h * chunk_q
                   + jnp.arange(chunk_q, dtype=jnp.int32)[None, :])
        fast_table = fast_rows(steps_q, positions)
        raw = jnp.einsum("cdqp,rpk->dcqrk", fast_table, frames, preferred_element_type=jnp.float32)
        raw = (raw * (1.0 / math.sqrt(positions))).astype(jnp.bfloat16)
        got = lax.all_to_all(raw, ("section", "scan"), 0, 0, tiled=True)
        got = got.reshape(section_count, scan_count, 2, chunk_q, rows_loc, rows_sec, detector_cols)
        spectrum = jnp.einsum("jiasb,sjcqibx->jicqax", matrices, got, preferred_element_type=jnp.float32)
        pieces.append(spectrum.astype(jnp.bfloat16).reshape(total_rows * 2 * chunk_q, detector_rows * detector_cols))
    slow_table = slow_matrix(jnp.arange(total_rows, dtype=jnp.int32), total_rows)
    slow_table = slow_table.transpose(0, 1, 3, 2).reshape(2 * total_rows, 2 * total_rows)
    return slow_and_filter(slow_table, pieces, wigner_filter, 1.0 / math.sqrt(total_rows))


def solution(mesh):
    in_specs = (
        P("scan", None, "section"),
        P("scan"),
        P(),
        P(None, None, ("section", "scan"), None),
    )
    out_specs = P(None, None, ("section", "scan"), None)
    return jax.shard_map(shards, mesh=mesh, in_specs=in_specs, out_specs=out_specs, check_vma=False)
```

```python
import math

import jax
import jax.numpy as jnp
from jax.experimental import pallas as pl
from jax.experimental.pallas import tpu as pltpu
from jax import lax
from jax.sharding import PartitionSpec as P

CHUNK_SIZES = (1, 1)


def fast_matrix(length):
    steps_p = jnp.arange(length, dtype=jnp.int32)
    phase = steps_p[:, None] * steps_p[None, :] % length
    angle = phase.astype(jnp.float32) * (2.0 * math.pi / length)
    return jnp.stack([jnp.cos(angle), -jnp.sin(angle)], axis=0).astype(jnp.bfloat16)


def fast_rows(steps_q, length):
    low = 32
    steps_low = jnp.arange(low, dtype=jnp.int32)
    steps_high = jnp.arange(length // low, dtype=jnp.int32) * low
    scale = 2.0 * math.pi / length
    angle_high = (steps_q[..., None] * steps_high % length).astype(jnp.float32) * scale
    angle_low = (steps_q[..., None] * steps_low % length).astype(jnp.float32) * scale
    cos_high, sin_high = jnp.cos(angle_high)[..., :, None], jnp.sin(angle_high)[..., :, None]
    cos_low, sin_low = jnp.cos(angle_low)[..., None, :], jnp.sin(angle_low)[..., None, :]
    cosine = cos_high * cos_low - sin_high * sin_low
    sine = sin_high * cos_low + cos_high * sin_low
    table = jnp.stack([cosine, -sine], axis=0)
    return table.reshape(table.shape[:-2] + (length,)).astype(jnp.bfloat16)


def slow_matrix(row_order, length):
    frequency = jnp.arange(length, dtype=jnp.int32)
    phase = frequency[:, None] * row_order[None, :] % length
    angle = phase.astype(jnp.float32) * (2.0 * math.pi / length)
    cosine = jnp.cos(angle)
    sine = jnp.sin(angle)
    upper = jnp.stack([cosine, sine], axis=1)
    lower = jnp.stack([-sine, cosine], axis=1)
    return jnp.stack([upper, lower], axis=0).astype(jnp.bfloat16)


def slow_kernel(table_ref, *refs, scale, sizes):
    chunks = len(sizes)
    spectrum_refs = refs[:chunks]
    gains_ref, out_ref, out_wide = refs[chunks:]
    q_loc = sum(sizes)
    half = gains_ref.shape[1] // q_loc
    depth = table_ref.shape[1]
    table = table_ref[...]
    for h in range(chunks):
        for k in range(sizes[h]):
            q = sum(sizes[:h]) + k
            rows = pl.ds(q, half, stride=q_loc)
            columns = spectrum_refs[h][pl.ds(k, depth, stride=sizes[h]), :]
            grid = jnp.dot(table, columns, preferred_element_type=jnp.float32) * scale
            grid_real = grid[:half]
            grid_imag = grid[half:]
            gain_real = gains_ref[0, rows, :].astype(jnp.float32)
            gain_imag = gains_ref[1, rows, :].astype(jnp.float32)
            out_wide[0, rows, :] = grid_real * gain_real - grid_imag * gain_imag
            out_wide[1, rows, :] = grid_real * gain_imag + grid_imag * gain_real
    out_ref[...] = out_wide[...].astype(out_ref.dtype)


def slow_and_filter(table, pieces, wigner_filter, scale):
    pixels = pieces[0].shape[1]
    shape = wigner_filter.shape
    flat = wigner_filter.reshape(shape[0], shape[1] * shape[2], shape[3])
    block = 128
    depth = table.shape[1]
    sizes = tuple(piece.shape[0] // depth for piece in pieces)
    out = pl.pallas_call(
        lambda *refs: slow_kernel(*refs, scale=scale, sizes=sizes),
        grid=(pixels // block,),
        in_specs=[pl.BlockSpec((depth, depth), lambda j: (0, 0))]
        + [pl.BlockSpec((piece.shape[0], block), lambda j: (0, j)) for piece in pieces]
        + [pl.BlockSpec((2, flat.shape[1], block), lambda j: (0, 0, j))],
        out_specs=pl.BlockSpec((2, flat.shape[1], block), lambda j: (0, 0, j)),
        out_shape=jax.ShapeDtypeStruct(flat.shape, jnp.bfloat16),
        scratch_shapes=[pltpu.VMEM((2, flat.shape[1], block), jnp.float32)],
    )(table, *pieces, flat)
    return out.reshape(shape)


def shards(frames, increments, resample, wigner_filter):
    section_count = lax.axis_size("section")
    scan_count = lax.axis_size("scan")
    devices = section_count * scan_count
    rows_loc, positions, pixels_loc = frames.shape
    total_rows = rows_loc * scan_count
    detector_rows = resample.shape[1]
    rows_sec = detector_rows // section_count
    detector_cols = pixels_loc // rows_sec
    q_loc = positions // devices
    sizes = tuple(q_loc * size // sum(CHUNK_SIZES) for size in CHUNK_SIZES)

    pieces = []
    for h, chunk_q in enumerate(sizes):
        steps_q = (jnp.arange(devices, dtype=jnp.int32)[:, None] * q_loc + sum(sizes[:h])
                   + jnp.arange(chunk_q, dtype=jnp.int32)[None, :])
        fast_table = fast_rows(steps_q, positions)
        if h == 1:
            fast_table, increments = lax.optimization_barrier((fast_table, increments))
            spread = jnp.broadcast_to(increments[None, :], (scan_count, rows_loc))
            every_increment = lax.all_to_all(spread, "scan", 0, 0, tiled=True).reshape(-1)
            shift_index = jnp.cumsum(every_increment) - 1
            matrices = resample[shift_index].reshape(scan_count, rows_loc, detector_rows, section_count, rows_sec)
        raw = jnp.einsum("cdqp,rpk->dcqrk", fast_table, frames, preferred_element_type=jnp.float32)
        raw = (raw * (1.0 / math.sqrt(positions))).astype(jnp.bfloat16)
        got = lax.all_to_all(raw, ("section", "scan"), 0, 0, tiled=True)
        pieces.append(got.reshape(section_count, scan_count, 2, chunk_q, rows_loc, rows_sec, detector_cols))
    for h, chunk_q in enumerate(sizes):
        spectrum = jnp.einsum("jiasb,sjcqibx->jicqax", matrices, pieces[h], preferred_element_type=jnp.float32)
        pieces[h] = spectrum.astype(jnp.bfloat16).reshape(total_rows * 2 * chunk_q, detector_rows * detector_cols)
    slow_table = slow_matrix(jnp.arange(total_rows, dtype=jnp.int32), total_rows)
    slow_table = slow_table.transpose(0, 1, 3, 2).reshape(2 * total_rows, 2 * total_rows)
    return slow_and_filter(slow_table, pieces, wigner_filter, 1.0 / math.sqrt(total_rows))


def solution(mesh):
    in_specs = (
        P("scan", None, "section"),
        P("scan"),
        P(),
        P(None, None, ("section", "scan"), None),
    )
    out_specs = P(None, None, ("section", "scan"), None)
    return jax.shard_map(shards, mesh=mesh, in_specs=in_specs, out_specs=out_specs, check_vma=False)
```

```python
import math

import jax
import jax.numpy as jnp
from jax.experimental import pallas as pl
from jax.experimental.pallas import tpu as pltpu
from jax import lax
from jax.sharding import PartitionSpec as P

CHUNK_SIZES = (1, 1)


def fast_matrix(length):
    steps_p = jnp.arange(length, dtype=jnp.int32)
    phase = steps_p[:, None] * steps_p[None, :] % length
    angle = phase.astype(jnp.float32) * (2.0 * math.pi / length)
    return jnp.stack([jnp.cos(angle), -jnp.sin(angle)], axis=0).astype(jnp.bfloat16)


def fast_rows(steps_q, length):
    low = 32
    steps_low = jnp.arange(low, dtype=jnp.int32)
    steps_high = jnp.arange(length // low, dtype=jnp.int32) * low
    scale = 2.0 * math.pi / length
    angle_high = (steps_q[..., None] * steps_high % length).astype(jnp.float32) * scale
    angle_low = (steps_q[..., None] * steps_low % length).astype(jnp.float32) * scale
    cos_high, sin_high = jnp.cos(angle_high)[..., :, None], jnp.sin(angle_high)[..., :, None]
    cos_low, sin_low = jnp.cos(angle_low)[..., None, :], jnp.sin(angle_low)[..., None, :]
    cosine = cos_high * cos_low - sin_high * sin_low
    sine = sin_high * cos_low + cos_high * sin_low
    table = jnp.stack([cosine, -sine], axis=0)
    return table.reshape(table.shape[:-2] + (length,)).astype(jnp.bfloat16)


def slow_matrix(row_order, length):
    frequency = jnp.arange(length, dtype=jnp.int32)
    phase = frequency[:, None] * row_order[None, :] % length
    angle = phase.astype(jnp.float32) * (2.0 * math.pi / length)
    cosine = jnp.cos(angle)
    sine = jnp.sin(angle)
    upper = jnp.stack([cosine, sine], axis=1)
    lower = jnp.stack([-sine, cosine], axis=1)
    return jnp.stack([upper, lower], axis=0).astype(jnp.bfloat16)


def slow_kernel(table_ref, *refs, scale, sizes):
    chunks = len(sizes)
    spectrum_refs = refs[:chunks]
    gains_ref, out_ref, out_wide = refs[chunks:]
    q_loc = sum(sizes)
    half = gains_ref.shape[2]
    depth = table_ref.shape[1]
    table = table_ref[...]
    for h in range(chunks):
        for k in range(sizes[h]):
            q = sum(sizes[:h]) + k
            rows = pl.ds(q, half, stride=q_loc)
            columns = spectrum_refs[h][pl.ds(k, depth, stride=sizes[h]), :]
            grid = jnp.dot(table, columns, preferred_element_type=jnp.float32) * scale
            grid_real = grid[:half]
            grid_imag = grid[half:]
            gain_real = gains_ref[0, q].astype(jnp.float32)
            gain_imag = gains_ref[1, q].astype(jnp.float32)
            out_wide[0, rows, :] = grid_real * gain_real - grid_imag * gain_imag
            out_wide[1, rows, :] = grid_real * gain_imag + grid_imag * gain_real
    out_ref[...] = out_wide[...].astype(out_ref.dtype)


def slow_and_filter(table, pieces, wigner_filter, scale):
    pixels = pieces[0].shape[1]
    shape = wigner_filter.shape
    flat = wigner_filter.reshape(shape[0], shape[1] * shape[2], shape[3])
    gains = wigner_filter.transpose(0, 2, 1, 3)
    block = 128
    depth = table.shape[1]
    sizes = tuple(piece.shape[0] // depth for piece in pieces)
    out = pl.pallas_call(
        lambda *refs: slow_kernel(*refs, scale=scale, sizes=sizes),
        grid=(pixels // block,),
        in_specs=[pl.BlockSpec((depth, depth), lambda j: (0, 0))]
        + [pl.BlockSpec((piece.shape[0], block), lambda j: (0, j)) for piece in pieces]
        + [pl.BlockSpec((2, shape[2], shape[1], block), lambda j: (0, 0, 0, j))],
        out_specs=pl.BlockSpec((2, flat.shape[1], block), lambda j: (0, 0, j)),
        out_shape=jax.ShapeDtypeStruct(flat.shape, jnp.bfloat16),
        scratch_shapes=[pltpu.VMEM((2, flat.shape[1], block), jnp.float32)],
    )(table, *pieces, gains)
    return out.reshape(shape)


def shards(frames, increments, resample, wigner_filter):
    section_count = lax.axis_size("section")
    scan_count = lax.axis_size("scan")
    devices = section_count * scan_count
    rows_loc, positions, pixels_loc = frames.shape
    total_rows = rows_loc * scan_count
    detector_rows = resample.shape[1]
    rows_sec = detector_rows // section_count
    detector_cols = pixels_loc // rows_sec
    q_loc = positions // devices
    sizes = tuple(q_loc * size // sum(CHUNK_SIZES) for size in CHUNK_SIZES)

    pieces = []
    for h, chunk_q in enumerate(sizes):
        steps_q = (jnp.arange(devices, dtype=jnp.int32)[:, None] * q_loc + sum(sizes[:h])
                   + jnp.arange(chunk_q, dtype=jnp.int32)[None, :])
        fast_table = fast_rows(steps_q, positions)
        if h == 1:
            fast_table, increments = lax.optimization_barrier((fast_table, increments))
            spread = jnp.broadcast_to(increments[None, :], (scan_count, rows_loc))
            every_increment = lax.all_to_all(spread, "scan", 0, 0, tiled=True).reshape(-1)
            shift_index = jnp.cumsum(every_increment) - 1
            matrices = resample[shift_index].reshape(scan_count, rows_loc, detector_rows, section_count, rows_sec)
        raw = jnp.einsum("cdqp,rpk->dcqrk", fast_table, frames, preferred_element_type=jnp.float32)
        raw = (raw * (1.0 / math.sqrt(positions))).astype(jnp.bfloat16)
        got = lax.all_to_all(raw, ("section", "scan"), 0, 0, tiled=True)
        pieces.append(got.reshape(section_count, scan_count, 2, chunk_q, rows_loc, rows_sec, detector_cols))
    for h, chunk_q in enumerate(sizes):
        spectrum = jnp.einsum("jiasb,sjcqibx->jicqax", matrices, pieces[h], preferred_element_type=jnp.float32)
        pieces[h] = spectrum.astype(jnp.bfloat16).reshape(total_rows * 2 * chunk_q, detector_rows * detector_cols)
    slow_table = slow_matrix(jnp.arange(total_rows, dtype=jnp.int32), total_rows)
    slow_table = slow_table.transpose(0, 1, 3, 2).reshape(2 * total_rows, 2 * total_rows)
    return slow_and_filter(slow_table, pieces, wigner_filter, 1.0 / math.sqrt(total_rows))


def solution(mesh):
    in_specs = (
        P("scan", None, "section"),
        P("scan"),
        P(),
        P(None, None, ("section", "scan"), None),
    )
    out_specs = P(None, None, ("section", "scan"), None)
    return jax.shard_map(shards, mesh=mesh, in_specs=in_specs, out_specs=out_specs, check_vma=False)
```

```python
import math

import jax
import jax.numpy as jnp
from jax.experimental import pallas as pl
from jax.experimental.pallas import tpu as pltpu
from jax import lax
from jax.sharding import PartitionSpec as P

CHUNK_SIZES = (1, 1)


def fast_matrix(length):
    steps_p = jnp.arange(length, dtype=jnp.int32)
    phase = steps_p[:, None] * steps_p[None, :] % length
    angle = phase.astype(jnp.float32) * (2.0 * math.pi / length)
    return jnp.stack([jnp.cos(angle), -jnp.sin(angle)], axis=0).astype(jnp.bfloat16)


def fast_rows(steps_q, length):
    low = 32
    steps_low = jnp.arange(low, dtype=jnp.int32)
    steps_high = jnp.arange(length // low, dtype=jnp.int32) * low
    scale = 2.0 * math.pi / length
    angle_high = (steps_q[..., None] * steps_high % length).astype(jnp.float32) * scale
    angle_low = (steps_q[..., None] * steps_low % length).astype(jnp.float32) * scale
    cos_high, sin_high = jnp.cos(angle_high)[..., :, None], jnp.sin(angle_high)[..., :, None]
    cos_low, sin_low = jnp.cos(angle_low)[..., None, :], jnp.sin(angle_low)[..., None, :]
    cosine = cos_high * cos_low - sin_high * sin_low
    sine = sin_high * cos_low + cos_high * sin_low
    table = jnp.stack([cosine, -sine], axis=0)
    return table.reshape(table.shape[:-2] + (length,)).astype(jnp.bfloat16)


def slow_matrix(row_order, length):
    frequency = jnp.arange(length, dtype=jnp.int32)
    phase = frequency[:, None] * row_order[None, :] % length
    angle = phase.astype(jnp.float32) * (2.0 * math.pi / length)
    cosine = jnp.cos(angle)
    sine = jnp.sin(angle)
    upper = jnp.stack([cosine, sine], axis=1)
    lower = jnp.stack([-sine, cosine], axis=1)
    return jnp.stack([upper, lower], axis=0).astype(jnp.bfloat16)


def slow_kernel(table_ref, *refs, scale, sizes):
    chunks = len(sizes)
    spectrum_refs = refs[:chunks]
    gains_ref, out_ref = refs[chunks:]
    half = gains_ref.shape[2]
    depth = table_ref.shape[1]
    table = table_ref[...]
    real_parts = []
    imag_parts = []
    for h in range(chunks):
        for k in range(sizes[h]):
            q = sum(sizes[:h]) + k
            columns = spectrum_refs[h][pl.ds(k, depth, stride=sizes[h]), :]
            grid = jnp.dot(table, columns, preferred_element_type=jnp.float32) * scale
            grid_real = grid[:half]
            grid_imag = grid[half:]
            gain_real = gains_ref[0, q].astype(jnp.float32)
            gain_imag = gains_ref[1, q].astype(jnp.float32)
            real_parts.append(grid_real * gain_real - grid_imag * gain_imag)
            imag_parts.append(grid_real * gain_imag + grid_imag * gain_real)
    width = out_ref.shape[2]
    out_ref[0] = jnp.stack(real_parts, axis=1).reshape(-1, width).astype(out_ref.dtype)
    out_ref[1] = jnp.stack(imag_parts, axis=1).reshape(-1, width).astype(out_ref.dtype)


def slow_and_filter(table, pieces, wigner_filter, scale):
    pixels = pieces[0].shape[1]
    shape = wigner_filter.shape
    flat = wigner_filter.reshape(shape[0], shape[1] * shape[2], shape[3])
    gains = wigner_filter.transpose(0, 2, 1, 3)
    block = 128
    depth = table.shape[1]
    sizes = tuple(piece.shape[0] // depth for piece in pieces)
    out = pl.pallas_call(
        lambda *refs: slow_kernel(*refs, scale=scale, sizes=sizes),
        grid=(pixels // block,),
        in_specs=[pl.BlockSpec((depth, depth), lambda j: (0, 0))]
        + [pl.BlockSpec((piece.shape[0], block), lambda j: (0, j)) for piece in pieces]
        + [pl.BlockSpec((2, shape[2], shape[1], block), lambda j: (0, 0, 0, j))],
        out_specs=pl.BlockSpec((2, flat.shape[1], block), lambda j: (0, 0, j)),
        out_shape=jax.ShapeDtypeStruct(flat.shape, jnp.bfloat16),
    )(table, *pieces, gains)
    return out.reshape(shape)


def shards(frames, increments, resample, wigner_filter):
    section_count = lax.axis_size("section")
    scan_count = lax.axis_size("scan")
    devices = section_count * scan_count
    rows_loc, positions, pixels_loc = frames.shape
    total_rows = rows_loc * scan_count
    detector_rows = resample.shape[1]
    rows_sec = detector_rows // section_count
    detector_cols = pixels_loc // rows_sec
    q_loc = positions // devices
    sizes = tuple(q_loc * size // sum(CHUNK_SIZES) for size in CHUNK_SIZES)

    pieces = []
    for h, chunk_q in enumerate(sizes):
        steps_q = (jnp.arange(devices, dtype=jnp.int32)[:, None] * q_loc + sum(sizes[:h])
                   + jnp.arange(chunk_q, dtype=jnp.int32)[None, :])
        fast_table = fast_rows(steps_q, positions)
        if h == 1:
            fast_table, increments = lax.optimization_barrier((fast_table, increments))
            spread = jnp.broadcast_to(increments[None, :], (scan_count, rows_loc))
            every_increment = lax.all_to_all(spread, "scan", 0, 0, tiled=True).reshape(-1)
            shift_index = jnp.cumsum(every_increment) - 1
            matrices = resample[shift_index].reshape(scan_count, rows_loc, detector_rows, section_count, rows_sec)
        raw = jnp.einsum("cdqp,rpk->dcqrk", fast_table, frames, preferred_element_type=jnp.float32)
        raw = (raw * (1.0 / math.sqrt(positions))).astype(jnp.bfloat16)
        got = lax.all_to_all(raw, ("section", "scan"), 0, 0, tiled=True)
        pieces.append(got.reshape(section_count, scan_count, 2, chunk_q, rows_loc, rows_sec, detector_cols))
    for h, chunk_q in enumerate(sizes):
        spectrum = jnp.einsum("jiasb,sjcqibx->jicqax", matrices, pieces[h], preferred_element_type=jnp.float32)
        pieces[h] = spectrum.astype(jnp.bfloat16).reshape(total_rows * 2 * chunk_q, detector_rows * detector_cols)
    slow_table = slow_matrix(jnp.arange(total_rows, dtype=jnp.int32), total_rows)
    slow_table = slow_table.transpose(0, 1, 3, 2).reshape(2 * total_rows, 2 * total_rows)
    return slow_and_filter(slow_table, pieces, wigner_filter, 1.0 / math.sqrt(total_rows))


def solution(mesh):
    in_specs = (
        P("scan", None, "section"),
        P("scan"),
        P(),
        P(None, None, ("section", "scan"), None),
    )
    out_specs = P(None, None, ("section", "scan"), None)
    return jax.shard_map(shards, mesh=mesh, in_specs=in_specs, out_specs=out_specs, check_vma=False)
```
